128 devices in a mesh: lr: 16 (over x, y), lc: 8 (over z, core).
Axes of the slice: x: 4, y: 4, z: 4, core: 2. Of those that a mesh axis runs over, the one named last changes fastest.
Arguments:
- queries: bfloat16 [8192, 768], P(('lr', 'lc')), may hold values from -6 to 6
- probes: int32 [8192, 16], P(('lr', 'lc')), may hold values from 0 to 1023, as said below
- assign: int32 [8192], P(('lr', 'lc')), may hold values from 0 to 1023, as said below
- list_rows: bfloat16 [1024, 1024, 768], P(('lr', 'lc')), may hold values from -0.21875 to 0.21875
- list_fill: int32 [1024], P(('lr', 'lc')), may hold values from 1 to 1024
- centroids: float32 [1024, 768], P(('lr', 'lc')), may hold values from -6 to 6
- list_sums: float32 [1024, 768], P(('lr', 'lc')), may hold values from -6 to 6
Outputs:
- dup_max: float32 [8192, 16], P(('lr', 'lc'))
- codes: bfloat16 [1024, 32, 768], P(('lr', 'lc'))
- scales: float32 [1024, 32], P(('lr', 'lc'))
- new_sums: float32 [1024, 768], P(('lr', 'lc'))
The draws below stay inside these ranges and needn't reach their ends.
Inputs may be any that keep to these rules, and one draw needn't show every extreme that they name: A list id is 8 times its owner's device index along lr+lc plus its place there. The probe pairs of one device's new vectors name lists of one owner at most 16 times, and one list is named by at most 256 pairs over all new vectors; both bounds are reached. A vector's probes may repeat a list. `assign`: one device's new vectors go to lists of one owner at most 2 times, and one list receives at most 32 new vectors; both bounds are reached.
All inputs are finite; a program needn't handle non-finite values. Where the reference program divides by a largest or mean magnitude, that divisor is 1e-20 or more.
Results may differ from the reference program's by a relative error of at most 0.001.
Values may be sent and summed in bfloat16 or wider, within the bound.
A program may use at most 64 MiB of HBM per device.

```python
import jax
import jax.numpy as jnp
from jax import lax

D = 768
PROBES = 16
Q_DEV = 64
L_DEV = 8
ROWS = 1024
QUERIES = 8192
LISTS = 1024
CAP = 16
CAP2 = 2
LIST_CAP = 256
APPEND = 32


def route_draw(key, device_count, item_count, capacity, list_count):
    hot_owner = jax.random.randint(jax.random.fold_in(key, 1), (), 0, device_count).astype(jnp.int32)
    offsets = jax.random.randint(jax.random.fold_in(key, 2), (device_count,), 0, list_count).astype(jnp.int32)

    def one_sender(sender):
        sender_key = jax.random.fold_in(jax.random.fold_in(key, 3), sender)
        shuffled = jax.random.permutation(jax.random.fold_in(sender_key, 4), (device_count - 1) * capacity).astype(jnp.int32)
        chosen = jnp.concatenate([jnp.arange(capacity, dtype=jnp.int32), shuffled[:item_count - capacity] + capacity])
        owner_rank = chosen // capacity
        other_index = owner_rank - 1
        others = other_index + (other_index >= hot_owner).astype(jnp.int32)
        owners = jnp.where(owner_rank == 0, hot_owner, others)
        within = chosen % capacity
        local_ids = (sender * capacity + within + offsets[owners]) % list_count
        list_ids = owners * list_count + local_ids
        reorder = jax.random.permutation(jax.random.fold_in(sender_key, 5), item_count)
        return list_ids[reorder].astype(jnp.int32)
    return jax.vmap(one_sender)(jnp.arange(device_count, dtype=jnp.int32))


def draw_probes(key, part):
    list_ids = route_draw(key, QUERIES // Q_DEV, Q_DEV * PROBES, CAP, L_DEV)
    return list_ids.reshape(QUERIES, PROBES)


def draw_assign(key, part):
    list_ids = route_draw(jax.random.fold_in(key, 7), QUERIES // Q_DEV, Q_DEV, CAP2, L_DEV)
    return list_ids.reshape(QUERIES)


def touch_ends(drawn, key, low, largest):
    index_at = [jax.random.randint(jax.random.fold_in(key, axis), (), 0, length) for axis, length in enumerate(drawn.shape)]
    longest = drawn.shape.index(max(drawn.shape))
    beside = index_at[:longest] + [(index_at[longest] + 1) % drawn.shape[longest]] + index_at[longest + 1:]
    return drawn.at[tuple(index_at)].set(low).at[tuple(beside)].set(largest)


def block_levels(key, shape, shards, low, largest):
    gain, own = 1.0, jax.random.fold_in(key, 6)
    for dim, parts in shards:
        draws = jnp.exp(jax.random.uniform(jax.random.fold_in(own, dim), (parts,), jnp.float32, low / len(shards), largest / len(shards)))
        gain = gain * jnp.repeat(draws, shape[dim] // parts).reshape([-1 if axis == dim else 1 for axis in range(len(shape))])
    return gain


def bell_draw(own_key, extent, spread, most, cuts=(), held_as=jnp.bfloat16):
    array = spread * jax.random.normal(own_key, extent, jnp.float32)
    if cuts:
        array = array * block_levels(own_key, extent, cuts, -0.22, 0.18)
    return jnp.clip(array, -most, most).astype(held_as)


def setup_inputs(seed: int = 0) -> dict:
    streams_of = jax.random.split(jax.random.key(seed), 8)
    queries = bell_draw(streams_of[0], (QUERIES, D), 1.0, 6.0, ((0, 128),))
    probes = draw_probes(jax.random.fold_in(streams_of[7], 71), 0)
    assign = draw_assign(jax.random.fold_in(streams_of[7], 71), 0)
    list_rows = bell_draw(streams_of[3], (LISTS, ROWS, D), D ** -0.5, 0.21875, ((0, 128),))
    list_fill = touch_ends(jax.random.randint(streams_of[4], (LISTS,), 1, ROWS + 1), jax.random.fold_in(streams_of[4], 1), 1, ROWS).astype(jnp.int32)
    centroids = bell_draw(streams_of[5], (LISTS, D), 1.0, 6.0, ((0, 128),), jnp.float32)
    list_sums = bell_draw(streams_of[6], (LISTS, D), 1.0, 6.0, ((0, 128),), jnp.float32)
    return dict(queries=queries, probes=probes, assign=assign, list_rows=list_rows, list_fill=list_fill, centroids=centroids, list_sums=list_sums)


def reference(queries, probes, assign, list_rows, list_fill, centroids, list_sums):
    pair_ids = probes.reshape(-1).astype(jnp.int32)
    pair_total = pair_ids.shape[0]
    sorted_order = jnp.argsort(pair_ids, stable=True).astype(jnp.int32)
    list_counts = jax.ops.segment_sum(jnp.ones_like(pair_ids), pair_ids, num_segments=LISTS).astype(jnp.int32)
    list_starts = (jnp.cumsum(list_counts) - list_counts).astype(jnp.int32)
    padded_order = jnp.concatenate([sorted_order, jnp.zeros((LIST_CAP,), jnp.int32)])

    def score_list(list_id):
        pair_index = lax.dynamic_slice_in_dim(padded_order, list_starts[list_id], LIST_CAP)
        live_slots = jnp.arange(LIST_CAP, dtype=jnp.int32) < list_counts[list_id]
        query_rows = queries[pair_index // PROBES]
        stored = list_rows[list_id]
        scores = jnp.dot(query_rows, stored.T, preferred_element_type=jnp.float32)
        scores = jnp.where(jnp.arange(ROWS, dtype=jnp.int32)[None, :] < list_fill[list_id], scores, -jnp.inf)
        best_scores = jnp.max(scores, axis=1)
        targets = jnp.where(live_slots, pair_index, pair_total).astype(jnp.int32)
        return best_scores, targets

    best_scores, targets = lax.map(score_list, jnp.arange(LISTS, dtype=jnp.int32))
    flat_best = jnp.zeros((pair_total,), jnp.float32).at[targets.reshape(-1)].set(best_scores.reshape(-1), mode="drop")
    dup_max = flat_best.reshape(QUERIES, PROBES)

    list_of = assign.astype(jnp.int32)
    residual = queries.astype(jnp.float32) - centroids[list_of]
    scale = jnp.max(jnp.abs(residual), axis=1) + 1e-6
    code_rows = (residual / scale[:, None]).astype(jnp.bfloat16)
    assign_order = jnp.argsort(list_of, stable=True).astype(jnp.int32)
    assign_counts = jax.ops.segment_sum(jnp.ones_like(list_of), list_of, num_segments=LISTS).astype(jnp.int32)
    assign_starts = (jnp.cumsum(assign_counts) - assign_counts).astype(jnp.int32)
    sorted_slot = jnp.arange(QUERIES, dtype=jnp.int32) - assign_starts[list_of[assign_order]]
    slot = jnp.zeros((QUERIES,), jnp.int32).at[assign_order].set(sorted_slot.astype(jnp.int32))
    position = list_of * APPEND + slot
    codes = jnp.zeros((LISTS * APPEND, D), jnp.bfloat16).at[position].set(code_rows).reshape(LISTS, APPEND, D)
    scales = jnp.zeros((LISTS * APPEND,), jnp.float32).at[position].set(scale).reshape(LISTS, APPEND)
    new_sums = list_sums + jax.ops.segment_sum(residual, list_of, num_segments=LISTS)
    return (dup_max, codes, scales, new_sums)
```

```python
import functools

import jax
import jax.numpy as jnp
from jax import lax
from jax.experimental import pallas as pl
from jax.experimental.pallas import tpu as pltpu
from jax.sharding import PartitionSpec as P

BF16, F32, I32 = jnp.bfloat16, jnp.float32, jnp.int32
ROW = (((1,), (1,)), ((), ()))
COL = (((0,), (0,)), ((), ()))


def iota(shape, axis):
    return lax.broadcasted_iota(I32, shape, axis)


def mask(cond):
    return jnp.where(cond, 1.0, 0.0).astype(BF16)


def mm(a, b, dims=(((1,), (0,)), ((), ()))):
    return lax.dot_general(a, b, dims, preferred_element_type=F32)


def split(x):
    hi = x.astype(BF16)
    rest = x - hi.astype(F32)
    mid = rest.astype(BF16)
    return hi, mid, (rest - mid.astype(F32)).astype(BF16)


def columns(table):
    return jnp.concatenate([table[:, j : j + 1] for j in range(table.shape[1])], axis=0)


def uncolumns(column, count):
    rows = column.shape[0] // count
    lane = iota((rows, count), 1)
    out = jnp.zeros((rows, count), column.dtype)
    for j in range(count):
        out = jnp.where(lane == j, column[j * rows : (j + 1) * rows], out)
    return out


def rank_by_owner(owners, group_size):
    count = owners.shape[0]
    hot = mask(owners == iota((count, group_size), 1))
    earlier = mask(iota((count, count), 1) < iota((count, count), 0))
    before = mm(earlier, hot)
    rank = jnp.sum(before * hot.astype(F32), axis=1, keepdims=True).astype(I32)
    return hot, rank


def route_kernel(probes_ref, assign_ref, table_ref, rank_ref, *, group_size, list_count, caps):
    cap, cap2 = caps
    query_count, probe_count = probes_ref.shape
    lists = columns(probes_ref[...])
    pair_count = query_count * probe_count
    hot, rank = rank_by_owner(lists // list_count, group_size)
    rank_ref[...] = uncolumns(rank, probe_count)
    lane = iota((pair_count, 128), 1)
    query = (iota((pair_count, 1), 0) % query_count).astype(F32)
    place = (lists % list_count + 1).astype(F32)
    values = jnp.where(lane == rank, query, 0.0) + jnp.where(lane == rank + cap, place, 0.0)
    table = mm(hot, values.astype(BF16), COL)

    ids = assign_ref[...]
    hot2, rank2 = rank_by_owner(ids // list_count, group_size)
    lane2 = iota((query_count, 128), 1) - 2 * cap
    query2 = iota((query_count, 1), 0).astype(F32)
    place2 = (ids % list_count + 1).astype(F32)
    values2 = jnp.where(lane2 == rank2, query2, 0.0) + jnp.where(lane2 == rank2 + cap2, place2, 0.0)
    table_ref[...] = table + mm(hot2, values2.astype(BF16), COL)


def score_kernel(fill_ref, lists_ref, vec_ref, rows_ref, best_ref, bucket_ref, *, per_list):
    which = pl.program_id(0)
    slots = lists_ref.shape[1]
    lanes = 128

    @pl.when(which == 0)
    def _():
        count = pl.num_programs(0)
        best_ref[...] = jnp.zeros_like(best_ref)
        before = mask(iota((lanes, lanes), 0) < iota((lanes, lanes), 1))
        seen = jnp.zeros((8, 1), F32)
        for block in range(slots // lanes):
            here = pl.ds(block * lanes, lanes)
            ids = lists_ref[:, here]
            hit = mask(ids == iota((8, lanes), 0) + 1)
            hit32 = hit.astype(F32)
            rank = mm(hit, before) + seen
            seen = seen + jnp.sum(hit32, axis=1, keepdims=True)
            rank = jnp.sum(rank * hit32, axis=0, keepdims=True).astype(I32)
            bucket_ref[:, here] = jnp.where(ids > 0, (ids - 1) * per_list + rank, count * per_list)

    select = mask(iota((per_list, slots), 0) == bucket_ref[...] - which * per_list)
    grouped = mm(select, vec_ref[...]).astype(BF16)
    scores = mm(rows_ref[0], grouped, ROW)
    scores = jnp.where(iota(scores.shape, 0) < fill_ref[which], scores, -jnp.inf)
    best = jnp.max(scores, axis=0, keepdims=True)
    hi, mid, low = [term.astype(F32) for term in split(best)]
    part = iota((8, per_list), 0)
    parts = jnp.where(part == 0, hi, jnp.where(part == 1, mid, jnp.where(part == 2, low, 0.0)))
    best_ref[...] += jnp.sum(mm(parts.astype(BF16), select), axis=0, keepdims=True)


def append_kernel(ids_ref, vec_ref, centroids_ref, sums_ref, codes_ref, scales_ref, out_ref, *, slots):
    count = ids_ref.shape[1]
    lists = centroids_ref.shape[0]
    ids = ids_ref[...]
    hit = mask(ids == iota((lists, count), 0) + 1)
    before = mask(iota((count, count), 0) < iota((count, count), 1))
    rank = jnp.sum(mm(hit, before) * hit.astype(F32), axis=0, keepdims=True).astype(I32)
    slot = jnp.where(ids > 0, (ids - 1) * slots + rank, lists * slots)
    center = sum(mm(hit, term, COL) for term in split(centroids_ref[...]))
    residual = vec_ref[...].astype(F32) - center
    scale = jnp.max(jnp.abs(residual), axis=1, keepdims=True) + 1e-06
    place = mask(iota((lists * slots, count), 0) == slot)
    codes_ref[...] = mm(place, (residual / scale).astype(BF16)).astype(BF16)
    wide = jnp.broadcast_to(scale, (count, 128))
    scales_ref[...] = sum(mm(place, term) for term in split(wide))[:, :1]
    out_ref[...] = sums_ref[...] + sum(mm(hit, term) for term in split(residual))


def pick_kernel(probes_ref, rank_ref, best_ref, out_ref, *, list_count):
    group_size, cap = best_ref.shape
    probe_count = probes_ref.shape[1]
    lists = columns(probes_ref[...])
    rank = columns(rank_ref[...])
    hot = mask(lists // list_count == iota((lists.shape[0], group_size), 1))
    found = sum(mm(hot, term) for term in split(best_ref[...]))
    mine = jnp.where(rank == iota(found.shape, 1), found, 0.0)
    out_ref[...] = uncolumns(jnp.sum(mine, axis=1, keepdims=True), probe_count)


def vmem(count):
    return [pl.BlockSpec(memory_space=pltpu.VMEM)] * count


def shape(dims, dtype):
    return jax.ShapeDtypeStruct(dims, dtype)


def exchange(x):
    return lax.all_to_all(x, ("lr", "lc"), split_axis=0, concat_axis=0, tiled=True)


def local(queries, probes, assign, list_rows, list_fill, centroids, list_sums):
    group_size = lax.axis_size("lr") * lax.axis_size("lc")
    list_count, row_count, feature_dim = list_rows.shape
    query_count, probe_count = probes.shape
    cap = 2 * query_count * probe_count // group_size
    cap2 = max(2, 2 * query_count // group_size)
    per_list = group_size * cap // list_count
    append_slots = group_size * cap2 // list_count
    slots, slots2 = group_size * cap, group_size * cap2

    table, rank = pl.pallas_call(
        functools.partial(
            route_kernel, group_size=group_size, list_count=list_count, caps=(cap, cap2)
        ),
        out_shape=(shape((group_size, 128), F32), shape((query_count, probe_count), I32)),
        in_specs=vmem(2),
        out_specs=tuple(vmem(2)),
        name="route",
    )(probes, assign[:, None])
    table = table.astype(I32)
    ids = jnp.concatenate([table[:, cap : 2 * cap], table[:, 2 * cap + cap2 : 2 * cap + 2 * cap2]], axis=1)

    def pick(which):
        hot = (which[:, :, None] == jnp.arange(query_count, dtype=I32)).astype(BF16)
        hot = hot.reshape(-1, query_count)
        picked = jnp.dot(hot, queries, preferred_element_type=F32).astype(BF16)
        return picked.reshape(group_size, -1, feature_dim)

    ids = exchange(ids)
    new = exchange(pick(table[:, 2 * cap : 2 * cap + cap2]))
    vectors = exchange(pick(table[:, :cap]))

    best = pl.pallas_call(
        functools.partial(score_kernel, per_list=per_list),
        grid=(list_count,),
        out_shape=shape((1, slots), F32),
        in_specs=[
            pl.BlockSpec(memory_space=pltpu.SMEM),
            pl.BlockSpec((1, slots), lambda i: (0, 0)),
            pl.BlockSpec((slots, feature_dim), lambda i: (0, 0)),
            pl.BlockSpec((1, row_count, feature_dim), lambda i: (i, 0, 0)),
        ],
        out_specs=pl.BlockSpec((1, slots), lambda i: (0, 0)),
        scratch_shapes=[pltpu.VMEM((1, slots), I32)],
        compiler_params=pltpu.CompilerParams(
            dimension_semantics=("arbitrary",), vmem_limit_bytes=48 << 20
        ),
        name="score",
    )(list_fill, ids[:, :cap].reshape(1, slots), vectors.reshape(slots, feature_dim), list_rows)

    codes, scales, sums = pl.pallas_call(
        functools.partial(append_kernel, slots=append_slots),
        out_shape=(
            shape((slots2, feature_dim), BF16),
            shape((slots2, 1), F32),
            shape((list_count, feature_dim), F32),
        ),
        in_specs=vmem(4),
        out_specs=tuple(vmem(3)),
        name="append",
    )(ids[:, cap:].reshape(1, slots2), new.reshape(slots2, feature_dim), centroids, list_sums)

    maxima = exchange(best.reshape(group_size, cap))
    dup_max = pl.pallas_call(
        functools.partial(pick_kernel, list_count=list_count),
        out_shape=shape((query_count, probe_count), F32),
        in_specs=vmem(3),
        out_specs=pl.BlockSpec(memory_space=pltpu.VMEM),
        name="pick",
    )(probes, rank, maxima)
    return (
        dup_max,
        codes.reshape(list_count, append_slots, feature_dim),
        scales.reshape(list_count, append_slots),
        sums,
    )


def solution(mesh):
    rows = P(("lr", "lc"), None)
    return jax.shard_map(
        local,
        mesh=mesh,
        in_specs=(rows, rows, P(("lr", "lc")), P(("lr", "lc"), None, None), P(("lr", "lc")), rows, rows),
        out_specs=(rows, P(("lr", "lc"), None, None), rows, rows),
        check_vma=False,
    )
```

```python
import functools

import jax
import jax.numpy as jnp
from jax import lax
from jax.experimental import pallas as pl
from jax.experimental.pallas import tpu as pltpu
from jax.sharding import PartitionSpec as P

BF16, F32, I32 = jnp.bfloat16, jnp.float32, jnp.int32
ROW = (((1,), (1,)), ((), ()))
COL = (((0,), (0,)), ((), ()))
SIDE = 4
MESH = pl.DeviceIdType.MESH
GROUPS = 8


def iota(shape, axis):
    return lax.broadcasted_iota(I32, shape, axis)


def mask(cond):
    return jnp.where(cond, 1.0, 0.0).astype(BF16)


def mm(a, b, dims=(((1,), (0,)), ((), ()))):
    return lax.dot_general(a, b, dims, preferred_element_type=F32)


def split(x):
    hi = x.astype(BF16)
    rest = x - hi.astype(F32)
    mid = rest.astype(BF16)
    return hi, mid, (rest - mid.astype(F32)).astype(BF16)


def columns(table):
    return jnp.concatenate([table[:, j : j + 1] for j in range(table.shape[1])], axis=0)


def uncolumns(column, count):
    rows = column.shape[0] // count
    lane = iota((rows, count), 1)
    out = jnp.zeros((rows, count), column.dtype)
    for j in range(count):
        out = jnp.where(lane == j, column[j * rows : (j + 1) * rows], out)
    return out


def rank_by_owner(owners, group_size):
    count = owners.shape[0]
    hot = mask(owners == iota((count, group_size), 1))
    earlier = mask(iota((count, count), 1) < iota((count, count), 0))
    before = mm(earlier, hot)
    rank = jnp.sum(before * hot.astype(F32), axis=1, keepdims=True).astype(I32)
    return hot, rank


def step_of(owner, me):
    x, y, z, c = me
    dx = (owner // 32 + SIDE - x) % SIDE
    dy = (owner // 8 + SIDE - y) % SIDE
    dz = (owner // 2 + SIDE - z) % SIDE
    dc = (owner + 2 - c) % 2
    return ((dz + SIDE - dx) % SIDE * 16 + (dy + SIDE - dx) % SIDE * 4 + dx) * 2 + dc


def offset_of(step):
    dx = step // 2 % SIDE
    return dx, (step // 8 + dx) % SIDE, (step // 32 + dx) % SIDE, step % 2


def position():
    lr, lc = lax.axis_index("lr"), lax.axis_index("lc")
    return lr // SIDE, lr % SIDE, lc // 2, lc % 2


def device(me, offset):
    x, y, z, c = [(own + far) % side for own, far, side in zip(me, offset, (SIDE, SIDE, SIDE, 2))]
    return x * SIDE + y, z * 2 + c


def route_kernel(probes_ref, assign_ref, table_ref, rank_ref, *, group_size, list_count, caps):
    cap, cap2 = caps
    me = position()
    query_count, probe_count = probes_ref.shape
    probes = probes_ref[...]
    pair_count = query_count * probe_count
    hot, rank = rank_by_owner(columns(step_of(probes // list_count, me)), group_size)
    rank_ref[...] = uncolumns(rank, probe_count)
    lane = iota((pair_count, 128), 1)
    query = columns(iota((query_count, probe_count), 0)).astype(F32)
    place = columns(probes % list_count + 1).astype(F32)
    values = jnp.where(lane == rank, query, 0.0) + jnp.where(lane == rank + cap, place, 0.0)
    table = mm(hot, values.astype(BF16), COL)

    ids = assign_ref[...]
    hot2, rank2 = rank_by_owner(step_of(ids // list_count, me), group_size)
    lane2 = iota((query_count, 128), 1) - 2 * cap
    query2 = iota((query_count, 1), 0).astype(F32)
    place2 = (ids % list_count + 1).astype(F32)
    values2 = jnp.where(lane2 == rank2, query2, 0.0) + jnp.where(lane2 == rank2 + cap2, place2, 0.0)
    table_ref[...] = table + mm(hot2, values2.astype(BF16), COL)


def arrival_order(slot, count):
    dx, dy, dz, dc = offset_of(slot % count)
    x, y, z, c = position()
    sx, sy, sz = [(own + SIDE - far) % SIDE for own, far in ((x, dx), (y, dy), (z, dz))]
    return (((sx * SIDE + sy) * SIDE + sz) * 2 + (c + 2 - dc) % 2) * 2 + slot // count


def append(ids, vectors, step_count, centroids, sums, codes_ref, scales_ref, out_ref):
    count = ids.shape[1]
    lists, slots = scales_ref.shape
    hit = mask(ids == iota((lists, count), 0) + 1)
    before = mask(arrival_order(iota((count, 1), 0), step_count) < arrival_order(iota((1, count), 1), step_count))
    rank = jnp.sum(mm(hit, before) * hit.astype(F32), axis=0, keepdims=True).astype(I32)
    slot = jnp.where(ids > 0, (ids - 1) * slots + rank, lists * slots)
    center = sum(mm(hit, term, COL) for term in split(centroids))
    residual = vectors.astype(F32) - center
    scale = jnp.max(jnp.abs(residual), axis=1, keepdims=True) + 1e-06
    place = mask(iota((lists * slots, count), 0) == slot)
    codes_ref[...] = mm(place, (residual / scale).astype(BF16)).astype(BF16)
    wide = jnp.broadcast_to(scale, (count, 128))
    placed = sum(mm(place, term) for term in split(wide))
    placed = jnp.where(iota((lists * slots, 1), 0) % slots == iota((1, 128), 1), placed, 0.0)
    block = mask(iota((lists, 1), 0) == iota((1, lists * slots), 1) // slots)
    scales_ref[...] = sum(mm(block, term) for term in split(placed))[:, :slots]
    out_ref[...] = sums + sum(mm(hit, term) for term in split(residual))


def pick(probes_ref, rank_ref, best, out_ref, list_count):
    group_size, cap = best.shape
    probe_count = probes_ref.shape[1]
    steps = columns(step_of(probes_ref[...] // list_count, position()))
    rank = columns(rank_ref[...])
    hot = mask(steps == iota((steps.shape[0], group_size), 1))
    found = sum(mm(hot, term) for term in split(best))
    mine = jnp.where(rank == iota(found.shape, 1), found, 0.0)
    out_ref[...] = uncolumns(jnp.sum(mine, axis=1, keepdims=True), probe_count)


def vmem(count):
    return [pl.BlockSpec(memory_space=pltpu.VMEM)] * count


def shape(dims, dtype):
    return jax.ShapeDtypeStruct(dims, dtype)


def routes(me):
    x, y, z, c = me
    xs, ys, zs = [[(own + far) % SIDE for far in range(SIDE)] for own in (x, y, z)]
    cores = [c, 1 - c]
    rows = [[xs[i] * SIDE + ys[j] for j in range(SIDE)] for i in range(SIDE)]
    cols = [[zs[k] * 2 + cores[l] for l in range(2)] for k in range(SIDE)]
    return lambda far: (rows[far[0]][far[1]], cols[far[2]][far[3]])


def greet(to, count):
    barrier = pltpu.get_barrier_semaphore()
    for step in range(1, count):
        pl.semaphore_signal(barrier, inc=1, device_id=to(offset_of(step)), device_id_type=MESH)
    pl.semaphore_wait(barrier, count - 1)


def buckets(lists, list_count, per_list):
    slots, lanes = lists.shape[1], 128
    before = mask(iota((lanes, lanes), 0) < iota((lanes, lanes), 1))
    seen = jnp.zeros((list_count, 1), F32)
    out = []
    for block in range(slots // lanes):
        ids = lists[:, block * lanes : (block + 1) * lanes]
        hit = mask(ids == iota((list_count, lanes), 0) + 1)
        hit32 = hit.astype(F32)
        rank = mm(hit, before) + seen
        seen = seen + jnp.sum(hit32, axis=1, keepdims=True)
        rank = jnp.sum(rank * hit32, axis=0, keepdims=True).astype(I32)
        out.append(jnp.where(ids > 0, (ids - 1) * per_list + rank, list_count * per_list))
    return jnp.concatenate(out, axis=1)


def ingest_kernel(
    fill_ref, probes_ref, rank_ref, ids_ref, new_ref, vec_ref, rows_ref, centroids_ref, sums_ref,
    dup_ref, codes_ref, scales_ref, out_ref,
    got_ids, got_new, got_vec, best_ref, got_best, rows, grouped, bucket_ref, row_ref,
    small_sem, vec_send, vec_recv, back_sem, rows_sem, own_sem,
    *, per_list,
):
    count, cap, feature_dim = vec_ref.shape
    list_count = rows_ref.shape[0]
    slots = count * cap
    each = count // GROUPS
    to = routes(position())
    steps = range(1, count)
    every = pl.ds(1, count - 1)
    near = (0, 0, 0, 1)

    def exchange(src, dst, send, recv, where, far):
        return pltpu.make_async_remote_copy(
            src_ref=src.at[where], dst_ref=dst.at[where], send_sem=send, recv_sem=recv,
            device_id=to(far), device_id_type=MESH,
        )

    def rows_copy(which):
        return pltpu.make_async_copy(rows_ref.at[which], rows.at[which], rows_sem.at[which])

    def own_copy(src, dst, i):
        return pltpu.make_async_copy(src.at[0], dst.at[0], own_sem.at[i])

    own = [own_copy(src, dst, i) for i, (src, dst) in enumerate(((ids_ref, got_ids), (new_ref, got_new), (vec_ref, got_vec)))]
    for copy in own:
        copy.start()
    for which in range(list_count):
        rows_copy(which).start()
    greet(to, count)
    for step in steps:
        exchange(ids_ref, got_ids, small_sem.at[0], small_sem.at[1], step, offset_of(step)).start()
    for step in steps:
        exchange(vec_ref, got_vec, vec_send, vec_recv.at[step // each], step, offset_of(step)).start()
        exchange(new_ref, got_new, small_sem.at[2], small_sem.at[3], step, offset_of(step)).start()

    grouped[...] = jnp.zeros_like(grouped)
    for copy in own:
        copy.wait()
    exchange(ids_ref, got_ids, small_sem.at[0], small_sem.at[1], every, near).wait()
    ids = got_ids[:, 0, :].astype(F32).T
    spread = mm(ids[:cap].astype(BF16), mask(iota((count, 1), 0) == iota((1, slots), 1) // cap))
    lists = jnp.where(iota((cap, 1), 0) == iota((1, slots), 1) % cap, spread, 0.0)
    lists = jnp.sum(lists, axis=0, keepdims=True).astype(I32)
    bucket_ref[...] = buckets(lists, list_count, per_list)

    for group in range(GROUPS):
        first = max(1, group * each)
        part = pl.ds(first, (group + 1) * each - first)
        exchange(vec_ref, got_vec, vec_send, vec_recv.at[group], part, near).wait_recv()
        bucket = bucket_ref[:, group * each * cap : (group + 1) * each * cap]

        @pl.loop(0, list_count)
        def _(which):
            here = pl.ds(pl.multiple_of(which * per_list, per_list), per_list)
            select = mask(iota((per_list, each * cap), 0) == bucket - which * per_list)
            vectors = got_vec[group * each : (group + 1) * each].reshape(each * cap, feature_dim)
            grouped[here] += mm(select, vectors).astype(BF16)

    row_ref[...] = jnp.zeros_like(row_ref)

    @pl.loop(0, list_count)
    def _(which):
        rows_copy(which).wait()
        here = pl.ds(pl.multiple_of(which * per_list, per_list), per_list)
        scores = mm(rows[which], grouped[here], ROW)
        scores = jnp.where(iota(scores.shape, 0) < fill_ref[which], scores, -jnp.inf)
        best = jnp.max(scores, axis=0, keepdims=True)
        hi, mid, low = [term.astype(F32) for term in split(best)]
        part = iota((8, per_list), 0)
        parts = jnp.where(part == 0, hi, jnp.where(part == 1, mid, jnp.where(part == 2, low, 0.0)))
        select = mask(iota((per_list, slots), 0) == bucket_ref[...] - which * per_list)
        row_ref[...] += jnp.sum(mm(parts.astype(BF16), select), axis=0, keepdims=True)

    mine = jnp.where(iota((cap, 1), 0) == iota((1, slots), 1) % cap, row_ref[...], 0.0)
    spot = mask(iota((count, 1), 0) == iota((1, slots), 1) // cap)
    best = sum(mm(term, spot, ROW) for term in split(mine))
    best = jnp.concatenate([best, jnp.zeros((128 - cap, count), F32)], axis=0)
    best_ref[...] = best.T[:, None, :]
    back_own = own_copy(best_ref, got_best, 0)
    back_own.start()
    for step in steps:
        far = offset_of(step)
        back = tuple((SIDE - d) % SIDE for d in far[:3]) + (far[3],)
        exchange(best_ref, got_best, back_sem.at[0], back_sem.at[1], step, back).start()

    exchange(new_ref, got_new, small_sem.at[2], small_sem.at[3], every, near).wait()
    exchange(vec_ref, got_vec, vec_send, vec_recv.at[0], every, near).wait_send()
    vectors = jnp.concatenate([got_new[:, k, :] for k in range(2)], axis=0)
    new_ids = jnp.concatenate([ids[cap + 2 + k : cap + 3 + k] for k in range(2)], axis=1).astype(I32)
    append(new_ids, vectors, count, centroids_ref[...], sums_ref[...], codes_ref, scales_ref, out_ref)
    back_own.wait()
    exchange(best_ref, got_best, back_sem.at[0], back_sem.at[1], every, near).wait()
    pick(probes_ref, rank_ref, got_best[:, 0, :cap], dup_ref, list_count)


def local(queries, probes, assign, list_rows, list_fill, centroids, list_sums):
    group_size = lax.axis_size("lr") * lax.axis_size("lc")
    list_count, row_count, feature_dim = list_rows.shape
    query_count, probe_count = probes.shape
    cap = 2 * query_count * probe_count // group_size
    cap2 = max(2, 2 * query_count // group_size)
    per_list = group_size * cap // list_count
    append_slots = group_size * cap2 // list_count
    slots, slots2 = group_size * cap, group_size * cap2

    table, rank = pl.pallas_call(
        functools.partial(
            route_kernel, group_size=group_size, list_count=list_count, caps=(cap, cap2)
        ),
        out_shape=(shape((group_size, 128), F32), shape((query_count, probe_count), I32)),
        in_specs=vmem(2),
        out_specs=tuple(vmem(2)),
        name="route",
    )(probes, assign[:, None])
    table = table.astype(I32)
    ids = jnp.pad(table[:, cap : 2 * cap + 2 * cap2], ((0, 0), (0, 128 - cap - 2 * cap2)))[:, None, :]

    def chosen(which):
        hot = (which[:, :, None] == jnp.arange(query_count, dtype=I32)).astype(BF16)
        hot = hot.reshape(-1, query_count)
        picked = jnp.dot(hot, queries, preferred_element_type=F32).astype(BF16)
        return picked.reshape(group_size, -1, feature_dim)

    buffers = [
        pltpu.VMEM((group_size, 1, 128), I32),
        pltpu.VMEM((group_size, cap2, feature_dim), BF16),
        pltpu.VMEM((group_size, cap, feature_dim), BF16),
        pltpu.VMEM((group_size, 1, 128), F32),
        pltpu.VMEM((group_size, 1, 128), F32),
        pltpu.VMEM((list_count, row_count, feature_dim), BF16),
        pltpu.VMEM((slots, feature_dim), BF16),
        pltpu.VMEM((1, slots), I32),
        pltpu.VMEM((1, slots), F32),
    ]
    DMA = pltpu.SemaphoreType.DMA
    dup_max, codes, scales, sums = pl.pallas_call(
        functools.partial(ingest_kernel, per_list=per_list),
        out_shape=(
            shape((query_count, probe_count), F32),
            shape((slots2, feature_dim), BF16),
            shape((list_count, append_slots), F32),
            shape((list_count, feature_dim), F32),
        ),
        in_specs=[
            pl.BlockSpec(memory_space=pltpu.SMEM),
            *vmem(5),
            pl.BlockSpec(memory_space=pl.ANY),
            *vmem(2),
        ],
        out_specs=tuple(vmem(4)),
        scratch_shapes=buffers
        + [DMA((4,)), DMA, DMA((GROUPS,)), DMA((2,)), DMA((list_count,)), DMA((3,))],
        compiler_params=pltpu.CompilerParams(
            collective_id=0, has_side_effects=True, vmem_limit_bytes=58 << 20
        ),
        name="ingest",
    )(
        list_fill, probes, rank, ids, chosen(table[:, 2 * cap : 2 * cap + cap2]),
        chosen(table[:, :cap]), list_rows, centroids, list_sums,
    )
    return dup_max, codes.reshape(list_count, append_slots, feature_dim), scales, sums


def solution(mesh):
    rows = P(("lr", "lc"), None)
    return jax.shard_map(
        local,
        mesh=mesh,
        in_specs=(rows, rows, P(("lr", "lc")), P(("lr", "lc"), None, None), P(("lr", "lc")), rows, rows),
        out_specs=(rows, P(("lr", "lc"), None, None), rows, rows),
        check_vma=False,
    )
```

```python
import functools

import jax
import jax.numpy as jnp
from jax import lax
from jax.experimental import pallas as pl
from jax.experimental.pallas import tpu as pltpu
from jax.sharding import PartitionSpec as P

BF16, F32, I32 = jnp.bfloat16, jnp.float32, jnp.int32
ROW = (((1,), (1,)), ((), ()))
COL = (((0,), (0,)), ((), ()))
SIDE = 4
MESH = pl.DeviceIdType.MESH
GROUPS = 8


def iota(shape, axis):
    return lax.broadcasted_iota(I32, shape, axis)


def mask(cond):
    return jnp.where(cond, 1.0, 0.0).astype(BF16)


def mm(a, b, dims=(((1,), (0,)), ((), ()))):
    return lax.dot_general(a, b, dims, preferred_element_type=F32)


def split(x):
    hi = x.astype(BF16)
    rest = x - hi.astype(F32)
    mid = rest.astype(BF16)
    return hi, mid, (rest - mid.astype(F32)).astype(BF16)


def eye(count):
    return iota((count, count), 0) == iota((count, count), 1)


def columns(table):
    own = eye(table.shape[1])
    turned = [jnp.where(own, table[j : j + 1], 0.0) for j in range(table.shape[0])]
    return jnp.concatenate([jnp.sum(one, axis=1, keepdims=True) for one in turned], axis=0)


def uncolumns(column, count):
    size = column.shape[0] // count
    own = eye(size)
    turned = [jnp.where(own, column[j * size : (j + 1) * size], 0.0) for j in range(count)]
    return jnp.concatenate([jnp.sum(one, axis=0, keepdims=True) for one in turned], axis=0)


def rank_by_owner(owners, group_size):
    count = owners.shape[0]
    hot = mask(owners == iota((count, group_size), 1))
    earlier = mask(iota((count, count), 1) < iota((count, count), 0))
    before = mm(earlier, hot)
    rank = jnp.sum(before * hot.astype(F32), axis=1, keepdims=True).astype(I32)
    return hot, rank


def step_of(owner, me):
    x, y, z, c = me
    dx = (owner // 32 + SIDE - x) % SIDE
    dy = (owner // 8 + SIDE - y) % SIDE
    dz = (owner // 2 + SIDE - z) % SIDE
    dc = (owner + 2 - c) % 2
    return ((dz + SIDE - dx) % SIDE * 16 + (dy + SIDE - dx) % SIDE * 4 + dx) * 2 + dc


def offset_of(step):
    dx = step // 2 % SIDE
    return dx, (step // 8 + dx) % SIDE, (step // 32 + dx) % SIDE, step % 2


def position():
    lr, lc = lax.axis_index("lr"), lax.axis_index("lc")
    return lr // SIDE, lr % SIDE, lc // 2, lc % 2


def device(me, offset):
    x, y, z, c = [(own + far) % side for own, far, side in zip(me, offset, (SIDE, SIDE, SIDE, 2))]
    return x * SIDE + y, z * 2 + c


def route_kernel(probes_ref, assign_ref, table_ref, ids_ref, rank_ref, *, group_size, list_count, caps):
    cap, cap2 = caps
    me = position()
    probe_count, query_count = probes_ref.shape
    probes = probes_ref[...]
    pair_count = query_count * probe_count
    hot, rank = rank_by_owner(columns(step_of(probes // list_count, me).astype(F32)).astype(I32), group_size)
    rank_ref[...] = uncolumns(rank.astype(F32), probe_count)
    lane = iota((pair_count, 128), 1)
    query = columns(iota((probe_count, query_count), 1).astype(F32))
    place = columns((probes % list_count + 1).astype(F32))
    values = jnp.where(lane == rank, query, 0.0) + jnp.where(lane == rank + cap, place, 0.0)
    table = mm(hot, values.astype(BF16), COL)

    ids = columns(assign_ref[...].astype(F32)).astype(I32)
    hot2, rank2 = rank_by_owner(step_of(ids // list_count, me), group_size)
    lane2 = iota((query_count, 128), 1) - 2 * cap
    query2 = iota((query_count, 1), 0).astype(F32)
    place2 = (ids % list_count + 1).astype(F32)
    values2 = jnp.where(lane2 == rank2, query2, 0.0) + jnp.where(lane2 == rank2 + cap2, place2, 0.0)
    table = (table + mm(hot2, values2.astype(BF16), COL)).astype(I32)
    table_ref[...] = table
    ids_ref[...] = table[:, None, :]


def arrival_order(slot, count):
    dx, dy, dz, dc = offset_of(slot % count)
    x, y, z, c = position()
    sx, sy, sz = [(own + SIDE - far) % SIDE for own, far in ((x, dx), (y, dy), (z, dz))]
    return (((sx * SIDE + sy) * SIDE + sz) * 2 + (c + 2 - dc) % 2) * 2 + slot // count


def append(ids, vectors, step_count, centroids, sums, codes_ref, scales_ref, out_ref):
    count = ids.shape[1]
    lists, slots = scales_ref.shape
    hit = mask(ids == iota((lists, count), 0) + 1)
    before = mask(arrival_order(iota((count, 1), 0), step_count) < arrival_order(iota((1, count), 1), step_count))
    rank = jnp.sum(mm(hit, before) * hit.astype(F32), axis=0, keepdims=True).astype(I32)
    slot = jnp.where(ids > 0, (ids - 1) * slots + rank, lists * slots)
    center = sum(mm(hit, term, COL) for term in split(centroids))
    residual = vectors.astype(F32) - center
    scale = jnp.max(jnp.abs(residual), axis=1, keepdims=True) + 1e-06
    place = mask(iota((lists * slots, count), 0) == slot)
    codes_ref[...] = mm(place, (residual / scale).astype(BF16)).astype(BF16)
    wide = jnp.broadcast_to(scale, (count, 128))
    placed = sum(mm(place, term) for term in split(wide))
    placed = jnp.where(iota((lists * slots, 1), 0) % slots == iota((1, 128), 1), placed, 0.0)
    block = mask(iota((lists, 1), 0) == iota((1, lists * slots), 1) // slots)
    scales_ref[...] = sum(mm(block, term) for term in split(placed))[:, :slots]
    out_ref[...] = sums + sum(mm(hit, term) for term in split(residual))


def finish_kernel(probes_ref, rank_ref, best_ref, codes_ref, scales_ref, sums_ref, dup_ref, *outs, list_count, cap):
    best = best_ref[:, :cap]
    steps = columns(step_of(probes_ref[...] // list_count, position()).astype(F32)).astype(I32)
    hot = mask(steps == iota((steps.shape[0], best.shape[0]), 1))
    found = sum(mm(hot, term) for term in split(best))
    mine = jnp.where(columns(rank_ref[...]) == iota(found.shape, 1).astype(F32), found, 0.0)
    dup_ref[...] = uncolumns(jnp.sum(mine, axis=1, keepdims=True), probes_ref.shape[0])
    for src, dst in zip((codes_ref, scales_ref, sums_ref), outs):
        dst[...] = src[...]


def vmem(count):
    return [pl.BlockSpec(memory_space=pltpu.VMEM)] * count


def shape(dims, dtype):
    return jax.ShapeDtypeStruct(dims, dtype)


def routes(me):
    x, y, z, c = me
    xs, ys, zs = [[(own + far) % SIDE for far in range(SIDE)] for own in (x, y, z)]
    cores = [c, 1 - c]
    rows = [[xs[i] * SIDE + ys[j] for j in range(SIDE)] for i in range(SIDE)]
    cols = [[zs[k] * 2 + cores[l] for l in range(2)] for k in range(SIDE)]
    return lambda far: (rows[far[0]][far[1]], cols[far[2]][far[3]])


def greet(to, count):
    barrier = pltpu.get_barrier_semaphore()
    for step in range(1, count):
        pl.semaphore_signal(barrier, inc=1, device_id=to(offset_of(step)), device_id_type=MESH)
    pl.semaphore_wait(barrier, count - 1)


def buckets(lists, list_count, per_list):
    slots, lanes = lists.shape[1], 128
    before = mask(iota((lanes, lanes), 0) < iota((lanes, lanes), 1))
    seen = jnp.zeros((list_count, 1), F32)
    out = []
    for block in range(slots // lanes):
        ids = lists[:, block * lanes : (block + 1) * lanes]
        hit = mask(ids == iota((list_count, lanes), 0) + 1)
        hit32 = hit.astype(F32)
        rank = mm(hit, before) + seen
        seen = seen + jnp.sum(hit32, axis=1, keepdims=True)
        rank = jnp.sum(rank * hit32, axis=0, keepdims=True).astype(I32)
        out.append(jnp.where(ids > 0, (ids - 1) * per_list + rank, list_count * per_list))
    return jnp.concatenate(out, axis=1)


def ingest_kernel(
    fill_ref, ids_ref, new_ref, vec_ref, rows_ref, centroids_ref, sums_ref,
    max_ref, codes_ref, scales_ref, out_ref,
    got_ids, got_new, got_vec, best_ref, got_best, rows, grouped, bucket_ref, bests_ref,
    small_sem, vec_send, vec_recv, back_sem, rows_sem, own_sem,
    *, per_list,
):
    count, cap, feature_dim = vec_ref.shape
    list_count = rows_ref.shape[0]
    slots = count * cap
    each = count // GROUPS
    to = routes(position())
    steps = range(1, count)
    every = pl.ds(1, count - 1)
    near = (0, 0, 0, 1)

    def exchange(src, dst, send, recv, where, far):
        return pltpu.make_async_remote_copy(
            src_ref=src.at[where], dst_ref=dst.at[where], send_sem=send, recv_sem=recv,
            device_id=to(far), device_id_type=MESH,
        )

    def rows_copy(which):
        return pltpu.make_async_copy(rows_ref.at[which], rows.at[which], rows_sem.at[which])

    def own_copy(src, dst, i):
        return pltpu.make_async_copy(src.at[0], dst.at[0], own_sem.at[i])

    own = [own_copy(src, dst, i) for i, (src, dst) in enumerate(((ids_ref, got_ids), (new_ref, got_new), (vec_ref, got_vec)))]
    for copy in own:
        copy.start()
    for which in range(list_count):
        rows_copy(which).start()
    greet(to, count)
    for step in steps:
        exchange(ids_ref, got_ids, small_sem.at[0], small_sem.at[1], step, offset_of(step)).start()
    for step in steps:
        exchange(vec_ref, got_vec, vec_send, vec_recv.at[step // each], step, offset_of(step)).start()
    for step in steps:
        exchange(new_ref, got_new, small_sem.at[2], small_sem.at[3], step, offset_of(step)).start()

    grouped[...] = jnp.zeros_like(grouped)
    for copy in own:
        copy.wait()
    exchange(ids_ref, got_ids, small_sem.at[0], small_sem.at[1], every, near).wait()
    ids = got_ids[:, 0, :].astype(F32).T
    spread = mm(ids[cap : 2 * cap].astype(BF16), mask(iota((count, 1), 0) == iota((1, slots), 1) // cap))
    lists = jnp.where(iota((cap, 1), 0) == iota((1, slots), 1) % cap, spread, 0.0)
    lists = jnp.sum(lists, axis=0, keepdims=True).astype(I32)
    bucket_ref[...] = buckets(lists, list_count, per_list)

    for group in range(GROUPS):
        first = max(1, group * each)
        part = pl.ds(first, (group + 1) * each - first)
        exchange(vec_ref, got_vec, vec_send, vec_recv.at[group], part, near).wait_recv()
        bucket = bucket_ref[:, group * each * cap : (group + 1) * each * cap]

        @pl.loop(0, list_count)
        def _(which):
            here = pl.ds(pl.multiple_of(which * per_list, per_list), per_list)
            select = mask(iota((per_list, each * cap), 0) == bucket - which * per_list)
            vectors = got_vec[group * each : (group + 1) * each].reshape(each * cap, feature_dim)
            grouped[here] += mm(select, vectors).astype(BF16)

    @pl.loop(0, list_count)
    def _(which):
        rows_copy(which).wait()
        here = pl.ds(pl.multiple_of(which * per_list, per_list), per_list)
        scores = mm(rows[which], grouped[here], ROW)
        scores = jnp.where(iota(scores.shape, 0) < fill_ref[which], scores, -jnp.inf)
        bests_ref[pl.ds(which, 1), :] = jnp.max(scores, axis=0, keepdims=True)

    bucket = bucket_ref[...]
    terms = jnp.concatenate([term.astype(F32) for term in split(bests_ref[...])], axis=0)
    found = mm(terms.astype(BF16), mask(iota((per_list, 1), 0) == bucket % per_list))
    found = sum(found[i * list_count : (i + 1) * list_count] for i in range(3))
    found = jnp.where(iota((list_count, 1), 0) == bucket // per_list, found, 0.0)
    found = jnp.sum(found, axis=0, keepdims=True)
    mine = jnp.where(iota((cap, 1), 0) == iota((1, slots), 1) % cap, found, 0.0)
    spot = mask(iota((count, 1), 0) == iota((1, slots), 1) // cap)
    best = sum(mm(term, spot, ROW) for term in split(mine))
    best = jnp.concatenate([best, jnp.zeros((128 - cap, count), F32)], axis=0)
    best_ref[...] = best.T[:, None, :]
    back_own = own_copy(best_ref, got_best, 0)
    back_own.start()
    for step in steps:
        far = offset_of(step)
        back = tuple((SIDE - d) % SIDE for d in far[:3]) + (far[3],)
        exchange(best_ref, got_best, back_sem.at[0], back_sem.at[1], step, back).start()

    exchange(new_ref, got_new, small_sem.at[2], small_sem.at[3], every, near).wait()
    exchange(vec_ref, got_vec, vec_send, vec_recv.at[0], every, near).wait_send()
    vectors = jnp.concatenate([got_new[:, k, :] for k in range(2)], axis=0)
    new_ids = jnp.concatenate([ids[2 * cap + 2 + k : 2 * cap + 3 + k] for k in range(2)], axis=1).astype(I32)
    append(new_ids, vectors, count, centroids_ref[...], sums_ref[...], codes_ref, scales_ref, out_ref)
    back_own.wait()
    exchange(best_ref, got_best, back_sem.at[0], back_sem.at[1], every, near).wait()
    max_ref[...] = got_best[:, 0, :]


def local(queries, probes, assign, list_rows, list_fill, centroids, list_sums):
    group_size = lax.axis_size("lr") * lax.axis_size("lc")
    list_count, row_count, feature_dim = list_rows.shape
    query_count, probe_count = probes.shape
    cap = 2 * query_count * probe_count // group_size
    cap2 = max(2, 2 * query_count // group_size)
    per_list = group_size * cap // list_count
    append_slots = group_size * cap2 // list_count
    slots, slots2 = group_size * cap, group_size * cap2

    probes = probes.T
    table, ids, rank = pl.pallas_call(
        functools.partial(
            route_kernel, group_size=group_size, list_count=list_count, caps=(cap, cap2)
        ),
        out_shape=(
            shape((group_size, 128), I32),
            shape((group_size, 1, 128), I32),
            shape((probe_count, query_count), F32),
        ),
        in_specs=vmem(2),
        out_specs=tuple(vmem(3)),
        name="route",
    )(probes, assign[None, :])

    def chosen(which):
        hot = (which[:, :, None] == jnp.arange(query_count, dtype=I32)).astype(BF16)
        hot = hot.reshape(-1, query_count)
        picked = jnp.dot(hot, queries, preferred_element_type=F32).astype(BF16)
        return picked.reshape(group_size, -1, feature_dim)

    buffers = [
        pltpu.VMEM((group_size, 1, 128), I32),
        pltpu.VMEM((group_size, cap2, feature_dim), BF16),
        pltpu.VMEM((group_size, cap, feature_dim), BF16),
        pltpu.VMEM((group_size, 1, 128), F32),
        pltpu.VMEM((group_size, 1, 128), F32),
        pltpu.VMEM((list_count, row_count, feature_dim), BF16),
        pltpu.VMEM((slots, feature_dim), BF16),
        pltpu.VMEM((1, slots), I32),
        pltpu.VMEM((list_count, per_list), F32),
    ]
    DMA = pltpu.SemaphoreType.DMA
    made = pl.pallas_call(
        functools.partial(ingest_kernel, per_list=per_list),
        out_shape=(
            shape((group_size, 128), F32),
            shape((slots2, feature_dim), BF16),
            shape((list_count, append_slots), F32),
            shape((list_count, feature_dim), F32),
        ),
        in_specs=[
            pl.BlockSpec(memory_space=pltpu.SMEM),
            *vmem(3),
            pl.BlockSpec(memory_space=pl.ANY),
            *vmem(2),
        ],
        out_specs=tuple(vmem(4)),
        scratch_shapes=buffers
        + [DMA((4,)), DMA, DMA((GROUPS,)), DMA((2,)), DMA((list_count,)), DMA((3,))],
        compiler_params=pltpu.CompilerParams(
            collective_id=0, has_side_effects=True, vmem_limit_bytes=58 << 20
        ),
        name="ingest",
    )(
        list_fill, ids, chosen(table[:, 2 * cap : 2 * cap + cap2]),
        chosen(table[:, :cap]), list_rows, centroids, list_sums,
    )
    dup_max, codes, scales, sums = pl.pallas_call(
        functools.partial(finish_kernel, list_count=list_count, cap=cap),
        out_shape=(
            shape((probe_count, query_count), F32),
            *[shape(one.shape, one.dtype) for one in made[1:]],
        ),
        in_specs=vmem(6),
        out_specs=tuple(vmem(4)),
        name="finish",
    )(probes, rank, *made)
    return dup_max.T, codes.reshape(list_count, append_slots, feature_dim), scales, sums


def solution(mesh):
    rows = P(("lr", "lc"), None)
    return jax.shard_map(
        local,
        mesh=mesh,
        in_specs=(rows, rows, P(("lr", "lc")), P(("lr", "lc"), None, None), P(("lr", "lc")), rows, rows),
        out_specs=(rows, P(("lr", "lc"), None, None), rows, rows),
        check_vma=False,
    )
```

```python
import functools

import jax
import jax.numpy as jnp
from jax import lax
from jax.experimental import pallas as pl
from jax.experimental.pallas import tpu as pltpu
from jax.sharding import PartitionSpec as P

BF16, F32, I32 = jnp.bfloat16, jnp.float32, jnp.int32
ROW = (((1,), (1,)), ((), ()))
COL = (((0,), (0,)), ((), ()))
SIDE = 4
MESH = pl.DeviceIdType.MESH
GROUPS = 8


def iota(shape, axis):
    return lax.broadcasted_iota(I32, shape, axis)


def mask(cond):
    return jnp.where(cond, 1.0, 0.0).astype(BF16)


def mm(a, b, dims=(((1,), (0,)), ((), ()))):
    return lax.dot_general(a, b, dims, preferred_element_type=F32)


def split(x):
    hi = x.astype(BF16)
    rest = x - hi.astype(F32)
    mid = rest.astype(BF16)
    return hi, mid, (rest - mid.astype(F32)).astype(BF16)


def eye(count):
    return iota((count, count), 0) == iota((count, count), 1)


def columns(table):
    own = eye(table.shape[1])
    turned = [jnp.where(own, table[j : j + 1], 0.0) for j in range(table.shape[0])]
    return jnp.concatenate([jnp.sum(one, axis=1, keepdims=True) for one in turned], axis=0)


def uncolumns(column, count):
    size = column.shape[0] // count
    own = eye(size)
    turned = [jnp.where(own, column[j * size : (j + 1) * size], 0.0) for j in range(count)]
    return jnp.concatenate([jnp.sum(one, axis=0, keepdims=True) for one in turned], axis=0)


def rank_by_owner(owners, group_size):
    count = owners.shape[0]
    hot = mask(owners == iota((count, group_size), 1))
    earlier = mask(iota((count, count), 1) < iota((count, count), 0))
    before = mm(earlier, hot)
    rank = jnp.sum(before * hot.astype(F32), axis=1, keepdims=True).astype(I32)
    return hot, rank


def step_of(owner, me):
    x, y, z, c = me
    dx = (owner // 32 + SIDE - x) % SIDE
    dy = (owner // 8 + SIDE - y) % SIDE
    dz = (owner // 2 + SIDE - z) % SIDE
    dc = (owner + 2 - c) % 2
    return ((dz + SIDE - dx) % SIDE * 16 + (dy + SIDE - dx) % SIDE * 4 + dx) * 2 + dc


def offset_of(step):
    dx = step // 2 % SIDE
    return dx, (step // 8 + dx) % SIDE, (step // 32 + dx) % SIDE, step % 2


def position():
    lr, lc = lax.axis_index("lr"), lax.axis_index("lc")
    return lr // SIDE, lr % SIDE, lc // 2, lc % 2


def device(me, offset):
    x, y, z, c = [(own + far) % side for own, far, side in zip(me, offset, (SIDE, SIDE, SIDE, 2))]
    return x * SIDE + y, z * 2 + c


def route_kernel(probes_ref, assign_ref, table_ref, ids_ref, rank_ref, *, group_size, list_count, caps):
    cap, cap2 = caps
    me = position()
    probe_count, query_count = probes_ref.shape
    probes = probes_ref[...]
    pair_count = query_count * probe_count
    hot, rank = rank_by_owner(columns(step_of(probes // list_count, me).astype(F32)).astype(I32), group_size)
    rank_ref[...] = uncolumns(rank.astype(F32), probe_count)
    lane = iota((pair_count, 128), 1)
    query = columns(iota((probe_count, query_count), 1).astype(F32))
    place = columns((probes % list_count + 1).astype(F32))
    values = jnp.where(lane == rank, query, 0.0) + jnp.where(lane == rank + cap, place, 0.0)
    table = mm(hot, values.astype(BF16), COL)

    ids = columns(assign_ref[...].astype(F32)).astype(I32)
    hot2, rank2 = rank_by_owner(step_of(ids // list_count, me), group_size)
    lane2 = iota((query_count, 128), 1) - 2 * cap
    query2 = iota((query_count, 1), 0).astype(F32)
    place2 = (ids % list_count + 1).astype(F32)
    values2 = jnp.where(lane2 == rank2, query2, 0.0) + jnp.where(lane2 == rank2 + cap2, place2, 0.0)
    table = (table + mm(hot2, values2.astype(BF16), COL)).astype(I32)
    table_ref[...] = table
    ids_ref[...] = table[:, None, :]


def arrival_order(slot, count):
    dx, dy, dz, dc = offset_of(slot % count)
    x, y, z, c = position()
    sx, sy, sz = [(own + SIDE - far) % SIDE for own, far in ((x, dx), (y, dy), (z, dz))]
    return (((sx * SIDE + sy) * SIDE + sz) * 2 + (c + 2 - dc) % 2) * 2 + slot // count


def append(ids, vectors, step_count, centroids, sums, codes_ref, scales_ref, out_ref):
    count = ids.shape[1]
    lists, slots = scales_ref.shape
    hit = mask(ids == iota((lists, count), 0) + 1)
    before = mask(arrival_order(iota((count, 1), 0), step_count) < arrival_order(iota((1, count), 1), step_count))
    rank = jnp.sum(mm(hit, before) * hit.astype(F32), axis=0, keepdims=True).astype(I32)
    slot = jnp.where(ids > 0, (ids - 1) * slots + rank, lists * slots)
    center = sum(mm(hit, term, COL) for term in split(centroids))
    residual = vectors.astype(F32) - center
    scale = jnp.max(jnp.abs(residual), axis=1, keepdims=True) + 1e-06
    place = mask(iota((lists * slots, count), 0) == slot)
    codes_ref[...] = mm(place, (residual / scale).astype(BF16)).astype(BF16)
    wide = jnp.broadcast_to(scale, (count, 128))
    placed = sum(mm(place, term) for term in split(wide))
    placed = jnp.where(iota((lists * slots, 1), 0) % slots == iota((1, 128), 1), placed, 0.0)
    block = mask(iota((lists, 1), 0) == iota((1, lists * slots), 1) // slots)
    scales_ref[...] = sum(mm(block, term) for term in split(placed))[:, :slots]
    out_ref[...] = sums + sum(mm(hit, term) for term in split(residual))


def finish_kernel(probes_ref, rank_ref, best_ref, codes_ref, scales_ref, sums_ref, dup_ref, *outs, list_count, cap):
    best = best_ref[:, :cap]
    steps = columns(step_of(probes_ref[...] // list_count, position()).astype(F32)).astype(I32)
    hot = mask(steps == iota((steps.shape[0], best.shape[0]), 1))
    found = sum(mm(hot, term) for term in split(best))
    mine = jnp.where(columns(rank_ref[...]) == iota(found.shape, 1).astype(F32), found, 0.0)
    dup_ref[...] = uncolumns(jnp.sum(mine, axis=1, keepdims=True), probes_ref.shape[0])
    for src, dst in zip((codes_ref, scales_ref, sums_ref), outs):
        dst[...] = src[...]


def vmem(count):
    return [pl.BlockSpec(memory_space=pltpu.VMEM)] * count


def shape(dims, dtype):
    return jax.ShapeDtypeStruct(dims, dtype)


def routes(me):
    x, y, z, c = me
    xs, ys, zs = [[(own + far) % SIDE for far in range(SIDE)] for own in (x, y, z)]
    cores = [c, 1 - c]
    rows = [[xs[i] * SIDE + ys[j] for j in range(SIDE)] for i in range(SIDE)]
    cols = [[zs[k] * 2 + cores[l] for l in range(2)] for k in range(SIDE)]
    return lambda far: (rows[far[0]][far[1]], cols[far[2]][far[3]])


def greet(to, count):
    barrier = pltpu.get_barrier_semaphore()
    for step in range(1, count):
        pl.semaphore_signal(barrier, inc=1, device_id=to(offset_of(step)), device_id_type=MESH)
    pl.semaphore_wait(barrier, count - 1)


def buckets(lists, list_count, per_list):
    slots, lanes = lists.shape[1], 128
    before = mask(iota((lanes, lanes), 0) < iota((lanes, lanes), 1))
    seen = jnp.zeros((list_count, 1), F32)
    out = []
    for block in range(slots // lanes):
        ids = lists[:, block * lanes : (block + 1) * lanes]
        hit = mask(ids == iota((list_count, lanes), 0) + 1)
        hit32 = hit.astype(F32)
        rank = mm(hit, before) + seen
        seen = seen + jnp.sum(hit32, axis=1, keepdims=True)
        rank = jnp.sum(rank * hit32, axis=0, keepdims=True).astype(I32)
        out.append(jnp.where(ids > 0, (ids - 1) * per_list + rank, list_count * per_list))
    return jnp.concatenate(out, axis=1)


def ingest_kernel(
    fill_ref, ids_ref, new_ref, vec_ref, rows_ref, centroids_ref, sums_ref,
    max_ref, codes_ref, scales_ref, out_ref,
    got_ids, got_new, got_vec, best_ref, got_best, rows, grouped, bucket_ref, bests_ref,
    small_sem, vec_send, vec_recv, back_sem, rows_sem, own_sem,
    *, per_list,
):
    count, cap, feature_dim = vec_ref.shape
    list_count = rows_ref.shape[0]
    slots = count * cap
    each = count // GROUPS
    to = routes(position())
    steps = range(1, count)
    every = pl.ds(1, count - 1)
    near = (0, 0, 0, 1)

    def exchange(src, dst, send, recv, where, far):
        return pltpu.make_async_remote_copy(
            src_ref=src.at[where], dst_ref=dst.at[where], send_sem=send, recv_sem=recv,
            device_id=to(far), device_id_type=MESH,
        )

    def rows_copy(which):
        return pltpu.make_async_copy(rows_ref.at[which], rows.at[which], rows_sem.at[which])

    def own_copy(src, dst, i):
        return pltpu.make_async_copy(src.at[0], dst.at[0], own_sem.at[i])

    own = [own_copy(src, dst, i) for i, (src, dst) in enumerate(((ids_ref, got_ids), (new_ref, got_new), (vec_ref, got_vec)))]
    for copy in own:
        copy.start()
    for which in range(list_count):
        rows_copy(which).start()
    greet(to, count)
    for step in steps:
        exchange(ids_ref, got_ids, small_sem.at[0], small_sem.at[1], step, offset_of(step)).start()
    for step in steps:
        exchange(vec_ref, got_vec, vec_send, vec_recv.at[step // each], step, offset_of(step)).start()
    for step in steps:
        exchange(new_ref, got_new, small_sem.at[2], small_sem.at[3], step, offset_of(step)).start()

    grouped[...] = jnp.zeros_like(grouped)
    for copy in own:
        copy.wait()
    exchange(ids_ref, got_ids, small_sem.at[0], small_sem.at[1], every, near).wait()
    ids = got_ids[:, 0, :].astype(F32).T
    spread = mm(ids[cap : 2 * cap].astype(BF16), mask(iota((count, 1), 0) == iota((1, slots), 1) // cap))
    lists = jnp.where(iota((cap, 1), 0) == iota((1, slots), 1) % cap, spread, 0.0)
    lists = jnp.sum(lists, axis=0, keepdims=True).astype(I32)
    bucket_ref[...] = buckets(lists, list_count, per_list)

    for group in range(GROUPS):
        first = max(1, group * each)
        part = pl.ds(first, (group + 1) * each - first)
        exchange(vec_ref, got_vec, vec_send, vec_recv.at[group], part, near).wait_recv()
        bucket = bucket_ref[:, group * each * cap : (group + 1) * each * cap]

        @pl.loop(0, list_count)
        def _(which):
            here = pl.ds(pl.multiple_of(which * per_list, per_list), per_list)
            select = mask(iota((per_list, each * cap), 0) == bucket - which * per_list)
            vectors = got_vec[group * each : (group + 1) * each].reshape(each * cap, feature_dim)
            grouped[here] += mm(select, vectors).astype(BF16)

    for which in range(list_count):
        rows_copy(which).wait()

    @pl.loop(0, list_count, unroll=4)
    def _(which):
        here = pl.ds(pl.multiple_of(which * per_list, per_list), per_list)
        scores = mm(rows[which], grouped[here], ROW)
        scores = jnp.where(iota(scores.shape, 0) < fill_ref[which], scores, -jnp.inf)
        bests_ref[pl.ds(which, 1), :] = jnp.max(scores, axis=0, keepdims=True)

    bucket = bucket_ref[...]
    terms = jnp.concatenate([term.astype(F32) for term in split(bests_ref[...])], axis=0)
    found = mm(terms.astype(BF16), mask(iota((per_list, 1), 0) == bucket % per_list))
    found = sum(found[i * list_count : (i + 1) * list_count] for i in range(3))
    found = jnp.where(iota((list_count, 1), 0) == bucket // per_list, found, 0.0)
    found = jnp.sum(found, axis=0, keepdims=True)
    mine = jnp.where(iota((cap, 1), 0) == iota((1, slots), 1) % cap, found, 0.0)
    spot = mask(iota((count, 1), 0) == iota((1, slots), 1) // cap)
    best = sum(mm(term, spot, ROW) for term in split(mine))
    best = jnp.concatenate([best, jnp.zeros((128 - cap, count), F32)], axis=0)
    best_ref[...] = best.T[:, None, :]
    back_own = own_copy(best_ref, got_best, 0)
    back_own.start()
    for step in steps:
        far = offset_of(step)
        back = tuple((SIDE - d) % SIDE for d in far[:3]) + (far[3],)
        exchange(best_ref, got_best, back_sem.at[0], back_sem.at[1], step, back).start()

    exchange(new_ref, got_new, small_sem.at[2], small_sem.at[3], every, near).wait()
    exchange(vec_ref, got_vec, vec_send, vec_recv.at[0], every, near).wait_send()
    vectors = jnp.concatenate([got_new[:, k, :] for k in range(2)], axis=0)
    new_ids = jnp.concatenate([ids[2 * cap + 2 + k : 2 * cap + 3 + k] for k in range(2)], axis=1).astype(I32)
    append(new_ids, vectors, count, centroids_ref[...], sums_ref[...], codes_ref, scales_ref, out_ref)
    back_own.wait()
    exchange(best_ref, got_best, back_sem.at[0], back_sem.at[1], every, near).wait()
    max_ref[...] = got_best[:, 0, :]


def local(queries, probes, assign, list_rows, list_fill, centroids, list_sums):
    group_size = lax.axis_size("lr") * lax.axis_size("lc")
    list_count, row_count, feature_dim = list_rows.shape
    query_count, probe_count = probes.shape
    cap = 2 * query_count * probe_count // group_size
    cap2 = max(2, 2 * query_count // group_size)
    per_list = group_size * cap // list_count
    append_slots = group_size * cap2 // list_count
    slots, slots2 = group_size * cap, group_size * cap2

    probes = probes.T
    table, ids, rank = pl.pallas_call(
        functools.partial(
            route_kernel, group_size=group_size, list_count=list_count, caps=(cap, cap2)
        ),
        out_shape=(
            shape((group_size, 128), I32),
            shape((group_size, 1, 128), I32),
            shape((probe_count, query_count), F32),
        ),
        in_specs=vmem(2),
        out_specs=tuple(vmem(3)),
        name="route",
    )(probes, assign[None, :])

    def chosen(which):
        hot = (which[:, :, None] == jnp.arange(query_count, dtype=I32)).astype(BF16)
        hot = hot.reshape(-1, query_count)
        picked = jnp.dot(hot, queries, preferred_element_type=F32).astype(BF16)
        return picked.reshape(group_size, -1, feature_dim)

    buffers = [
        pltpu.VMEM((group_size, 1, 128), I32),
        pltpu.VMEM((group_size, cap2, feature_dim), BF16),
        pltpu.VMEM((group_size, cap, feature_dim), BF16),
        pltpu.VMEM((group_size, 1, 128), F32),
        pltpu.VMEM((group_size, 1, 128), F32),
        pltpu.VMEM((list_count, row_count, feature_dim), BF16),
        pltpu.VMEM((slots, feature_dim), BF16),
        pltpu.VMEM((1, slots), I32),
        pltpu.VMEM((list_count, per_list), F32),
    ]
    DMA = pltpu.SemaphoreType.DMA
    made = pl.pallas_call(
        functools.partial(ingest_kernel, per_list=per_list),
        out_shape=(
            shape((group_size, 128), F32),
            shape((slots2, feature_dim), BF16),
            shape((list_count, append_slots), F32),
            shape((list_count, feature_dim), F32),
        ),
        in_specs=[
            pl.BlockSpec(memory_space=pltpu.SMEM),
            *vmem(3),
            pl.BlockSpec(memory_space=pl.ANY),
            *vmem(2),
        ],
        out_specs=tuple(vmem(4)),
        scratch_shapes=buffers
        + [DMA((4,)), DMA, DMA((GROUPS,)), DMA((2,)), DMA((list_count,)), DMA((3,))],
        compiler_params=pltpu.CompilerParams(
            collective_id=0, has_side_effects=True, vmem_limit_bytes=58 << 20
        ),
        name="ingest",
    )(
        list_fill, ids, chosen(table[:, 2 * cap : 2 * cap + cap2]),
        chosen(table[:, :cap]), list_rows, centroids, list_sums,
    )
    dup_max, codes, scales, sums = pl.pallas_call(
        functools.partial(finish_kernel, list_count=list_count, cap=cap),
        out_shape=(
            shape((probe_count, query_count), F32),
            *[shape(one.shape, one.dtype) for one in made[1:]],
        ),
        in_specs=vmem(6),
        out_specs=tuple(vmem(4)),
        name="finish",
    )(probes, rank, *made)
    return dup_max.T, codes.reshape(list_count, append_slots, feature_dim), scales, sums


def solution(mesh):
    rows = P(("lr", "lc"), None)
    return jax.shard_map(
        local,
        mesh=mesh,
        in_specs=(rows, rows, P(("lr", "lc")), P(("lr", "lc"), None, None), P(("lr", "lc")), rows, rows),
        out_specs=(rows, P(("lr", "lc"), None, None), rows, rows),
        check_vma=False,
    )
```
